32 devices in a mesh: pano: 2 (over y), seq: 4 (over z), win: 4 (over x, core).
Axes of the slice: x: 2, y: 2, z: 4, core: 2. Of those that a mesh axis runs over, the one named last changes fastest.
Arguments:
- query: bfloat16 [8, 768, 1536], P(('pano', 'win'), 'seq'), parts along dimension 0, may hold values from -8 to 8
- key_image: bfloat16 [8, 768, 1536], P(('pano', 'win'), 'seq'), parts along dimension 0, may hold values from -8 to 8
- value_image: bfloat16 [8, 768, 1536], P(('pano', 'win'), 'seq'), parts along dimension 0, may hold values from -6 to 6
- key_text: bfloat16 [8, 64, 1536], P(('pano', 'win'), 'seq'), parts along dimension 0, may hold values from -6 to 6
- value_text: bfloat16 [8, 64, 1536], P(('pano', 'win'), 'seq'), parts along dimension 0, may hold values from -6 to 6
- prompt_ids: int32 [8, 64], P(('pano', 'win')), parts along dimension 0, may hold values from 0 to 32127, as said below
- blend: int32 [8, 768], P(('pano', 'win'), 'seq'), parts along dimension 0, may hold values from 1 to 15, as said below
- w_out: bfloat16 [1536, 3072], replicated, may hold values from -0.15625 to 0.15625
Outputs:
- joined: bfloat16 [8, 768, 3072], P(('pano', 'win'), 'seq'), parts along dimension 0
The draws below stay inside these ranges and needn't reach their ends.
There are 2 independent parts, one for each index of `pano`. The reference program is written for one: setup_inputs(seed, part) draws one part's arguments, and reference() takes and returns one part's arrays. A program takes and returns all parts, laid end to end along the dimension named above; an argument that names none is the same for every part. Nothing has to cross between parts.
Inputs may be any that keep to these rules, and one draw needn't show every extreme that they name: `prompt_ids`: in each window the nonzero ids form a leading run of 16 or more positions and the rest are 0. At row r and column c < 32, blend[w] plus blend[w - 1] at row r, column c + 32 equals 16, window numbers taken modulo 4.
All inputs are finite; a program needn't handle non-finite values.
Results may differ from the reference program's by a relative error of at most 0.0085.
Values may be sent and summed in bfloat16 or wider, within the bound.
A program may use at most 64 MiB of HBM per device.

```python
import jax
import jax.numpy as jnp
from jax import lax

D = 3072
HEADS = 12
HEAD_DIM = 128
VOCAB = 32128
WCOLS = 64
STRIDE = 32
WROWS = 12
IMG = 768
TXT = 64
HD = 1536
WINDOWS = 4


def draw_query(key, part):
    shape_full = (WINDOWS, IMG, HEADS * HEAD_DIM)
    values = jnp.clip(2.5 * jax.random.normal(jax.random.fold_in(key, 23), shape_full, jnp.float32), -8.0, 8.0)
    return values.astype(jnp.bfloat16)


def draw_key_image(key, part):
    shape_full = (WINDOWS, IMG, HEADS * HEAD_DIM)
    values = jnp.clip(jax.random.normal(jax.random.fold_in(key, 33), shape_full, jnp.float32), -6.0, 6.0)
    return values.astype(jnp.bfloat16)


def draw_prompt_ids(key, part):
    lengths = jax.random.randint(jax.random.fold_in(key, 41), (WINDOWS, 1), TXT // 4, TXT + 1)
    tokens = jax.random.randint(jax.random.fold_in(key, 42), (WINDOWS, TXT), 1, VOCAB)
    position = jnp.arange(TXT)[None, :]
    return jnp.where(position < lengths, tokens, 0).astype(jnp.int32)


def draw_blend(key, part):
    ramps = jax.random.randint(jax.random.fold_in(key, 51), (WINDOWS, WROWS, STRIDE), 1, 16)
    left_part = jnp.roll(ramps, 1, axis=0)
    right_part = 16 - ramps
    return jnp.concatenate([left_part, right_part], axis=2).reshape(WINDOWS, IMG).astype(jnp.int32)


def level_of(rng, dims, pieces, low, high):
    def one(axis_at, blocks):
        heights = jax.random.uniform(jax.random.fold_in(jax.random.fold_in(rng, 6), axis_at), (blocks,), jnp.float32, low / len(pieces), high / len(pieces))
        return jnp.repeat(jnp.exp(heights), dims[axis_at] // blocks).reshape((-1,) + (1,) * (len(dims) - axis_at - 1))

    loudness = one(*pieces[0])
    for cut in pieces[1:]:
        loudness = loudness * one(*cut)
    return loudness


def gaussian(rng, extent, spread, limit, shards=(), kind=jnp.bfloat16):
    array = jax.random.normal(rng, extent, jnp.float32) * spread
    if len(shards) > 0:
        array = level_of(rng, extent, shards, -0.22, 0.18) * array
    return jnp.clip(array, min=-limit, max=limit).astype(kind)


def setup_inputs(seed: int = 0, part: int = 0) -> dict:
    streams_of = jax.random.split(jax.random.key(seed), 9)
    own_keys = jax.random.split(jax.random.fold_in(streams_of[8], part), 9)
    query = draw_query(jax.random.fold_in(jax.random.fold_in(streams_of[8], part), 71), part)
    key_image = draw_key_image(jax.random.fold_in(jax.random.fold_in(streams_of[8], part), 71), part)
    value_image = gaussian(own_keys[2], (WINDOWS, IMG, HD), 1.0, 6.0, ((0, 4), (1, 4)))
    key_text = gaussian(own_keys[3], (WINDOWS, TXT, HD), 1.0, 6.0, ((0, 4), (1, 4)))
    value_text = gaussian(own_keys[4], (WINDOWS, TXT, HD), 1.0, 6.0, ((0, 4), (1, 4)))
    prompt_ids = draw_prompt_ids(jax.random.fold_in(jax.random.fold_in(streams_of[8], part), 71), part)
    blend = draw_blend(jax.random.fold_in(jax.random.fold_in(streams_of[8], part), 71), part)
    w_out = gaussian(streams_of[7], (HD, D), HD ** -0.5, 0.15625)
    return dict(query=query, key_image=key_image, value_image=value_image, key_text=key_text, value_text=value_text, prompt_ids=prompt_ids, blend=blend, w_out=w_out)


blend_total = 16.0


def attend_window(operands):
    query, key_image, value_image, key_text, value_text, prompt_ids = operands
    keys_all = jnp.concatenate([key_image, key_text], axis=0)
    values_all = jnp.concatenate([value_image, value_text], axis=0)
    valid_keys = jnp.concatenate([jnp.ones((IMG,), jnp.bool_), prompt_ids != 0])

    def one_head(head_index):
        offset = (head_index * HEAD_DIM).astype(jnp.int32)
        query_head = lax.dynamic_slice_in_dim(query, offset, HEAD_DIM, 1)
        key_head = lax.dynamic_slice_in_dim(keys_all, offset, HEAD_DIM, 1)
        value_head = lax.dynamic_slice_in_dim(values_all, offset, HEAD_DIM, 1)
        scores = jnp.dot(query_head, key_head.T, preferred_element_type=jnp.float32) * (HEAD_DIM ** -0.5)
        scores = jnp.where(valid_keys[None, :], scores, -jnp.inf)
        peak = jnp.max(scores, axis=1, keepdims=True)
        weights = jnp.exp(scores - peak)
        total = jnp.sum(weights, axis=1, keepdims=True)
        return jnp.dot(weights.astype(jnp.bfloat16), value_head, preferred_element_type=jnp.float32) / total

    heads_out = lax.map(one_head, jnp.arange(HEADS, dtype=jnp.int32))
    return jnp.transpose(heads_out, (1, 0, 2)).reshape(IMG, HD).astype(jnp.bfloat16)


def reference(query, key_image, value_image, key_text, value_text, prompt_ids, blend, w_out):
    attended = lax.map(attend_window, (query, key_image, value_image, key_text, value_text, prompt_ids))
    projected = jnp.dot(attended.reshape(WINDOWS * IMG, HD), w_out, preferred_element_type=jnp.float32)
    projected = projected.astype(jnp.bfloat16).reshape(WINDOWS, WROWS, WCOLS, D)
    prev_right = jnp.roll(projected[:, :, STRIDE:], 1, axis=0)
    next_left = jnp.roll(projected[:, :, :STRIDE], -1, axis=0)
    partner = jnp.concatenate([prev_right, next_left], axis=2).astype(jnp.float32)
    weight_own = blend.reshape(WINDOWS, WROWS, WCOLS, 1).astype(jnp.float32)
    joined = (weight_own * projected.astype(jnp.float32) + (blend_total - weight_own) * partner) / blend_total
    return joined.astype(jnp.bfloat16).reshape(WINDOWS, IMG, D)
```

```python
import functools

import jax
import jax.numpy as jnp
from jax import lax
from jax.experimental import pallas as pl
from jax.experimental.pallas import tpu as pltpu
from jax.sharding import PartitionSpec as P

HEADS = 12
HEAD_DIM = 128
WCOLS = 64
ROWS_DEV = 3
STRIDE = 32


blend_total = 16.0


def swapped(block, axis, stride):
    count = lax.axis_size(axis)
    route = []
    for low in range(count):
        high = low | 1 << stride
        if high != low and high < count:
            route += [(low, high), (high, low)]
    return lax.ppermute(block, axis, route)


def shifted(block, axis, distance):
    devices = range(lax.axis_size(axis))
    route = [((i - distance) % len(devices), i) for i in devices]
    return lax.ppermute(block, axis, route)


def regroup(stacked, bit_count):
    row_count = stacked.shape[0]
    carried = stacked.reshape(row_count, 1 << bit_count, -1)
    position = lax.axis_index("seq")
    for bit_index in range(bit_count):
        own_bit = position >> bit_index & 1
        paired = carried.reshape(carried.shape[0], carried.shape[1] // 2, 2, carried.shape[2])
        kept_half = lax.dynamic_index_in_dim(paired, own_bit, 2, keepdims=False)
        sent_half = lax.dynamic_index_in_dim(paired, 1 - own_bit, 2, keepdims=False)
        received = swapped(sent_half, "seq", bit_index)
        lower_half = jnp.where(own_bit == 0, kept_half, received)
        upper_half = jnp.where(own_bit == 0, received, kept_half)
        carried = jnp.concatenate([lower_half, upper_half], axis=0)
    return carried.reshape(carried.shape[0], -1)


def ungroup(attended, bit_count):
    carried = attended.reshape(attended.shape[0], 1, attended.shape[1])
    position = lax.axis_index("seq")
    for bit_index in reversed(range(bit_count)):
        own_bit = position >> bit_index & 1
        halves = carried.reshape(2, carried.shape[0] // 2, carried.shape[1], carried.shape[2])
        kept_half = lax.dynamic_index_in_dim(halves, own_bit, 0, keepdims=False)
        sent_half = lax.dynamic_index_in_dim(halves, 1 - own_bit, 0, keepdims=False)
        received = swapped(sent_half, "seq", bit_index)
        lower_half = jnp.where(own_bit == 0, kept_half, received)
        upper_half = jnp.where(own_bit == 0, received, kept_half)
        stacked = jnp.stack([lower_half, upper_half], axis=2)
        carried = stacked.reshape(kept_half.shape[0], -1, kept_half.shape[2])
    return carried.reshape(carried.shape[0], -1)


def absorb(carried, key_value, valid_keys, queries, head_count):
    running, denominator, numerator = carried
    keys_block = key_value[0].reshape(key_value.shape[1], head_count, HEAD_DIM)
    values_block = key_value[1].reshape(key_value.shape[1], head_count, HEAD_DIM)
    scores = jnp.einsum(
        "qhd,khd->qhk", queries, keys_block, preferred_element_type=jnp.float32
    ) * HEAD_DIM ** (-0.5)
    scores = jnp.where(valid_keys[None, None, :], scores, -jnp.inf)
    updated = jnp.maximum(running, jnp.max(scores, axis=2))
    rescale = jnp.exp(running - updated)
    weights = jnp.exp(scores - updated[:, :, None])
    denominator = denominator * rescale + jnp.sum(weights, axis=2)
    product = jnp.einsum(
        "qhk,khd->qhd",
        weights.astype(jnp.bfloat16),
        values_block,
        preferred_element_type=jnp.float32,
    )
    numerator = numerator * rescale[:, :, None] + product
    return (updated, denominator, numerator)


def pass_strips(window_rows):
    from_prev = shifted(window_rows[:, STRIDE:], "win", 1)
    from_next = shifted(window_rows[:, :STRIDE], "win", -1)
    return (from_prev, from_next)


def project_rows(features, w_out):
    flat_rows = features.reshape(-1, features.shape[-1])
    result = jnp.dot(flat_rows, w_out, preferred_element_type=jnp.float32).astype(jnp.bfloat16)
    return result.reshape(ROWS_DEV, -1, w_out.shape[1])


def on_device(query, key_image, value_image, key_text, value_text, prompt_ids, blend, w_out):
    bit_count = 2
    group_size = 1 << bit_count
    image_rows = query.shape[1]
    text_rows = key_text.shape[1]
    key_rows = image_rows + text_rows
    head_count = HEADS // group_size
    stacked = jnp.concatenate(
        [query[0], key_image[0], key_text[0], value_image[0], value_text[0]], axis=0
    )
    grouped = regroup(stacked, bit_count).reshape(group_size, image_rows + 2 * key_rows, -1)
    queries = grouped[:, :image_rows].reshape(group_size * image_rows, head_count, HEAD_DIM)
    keys_grouped = grouped[:, image_rows : image_rows + key_rows].reshape(group_size * key_rows, -1)
    values_grouped = grouped[:, image_rows + key_rows :].reshape(group_size * key_rows, -1)
    key_value = jnp.stack([keys_grouped, values_grouped])
    seq_count = lax.axis_size("seq")
    text_valid = prompt_ids[0].reshape(seq_count, text_rows) != 0
    key_valid = jnp.concatenate([jnp.ones((seq_count, image_rows), jnp.bool_), text_valid], axis=1)
    group_count = seq_count // group_size
    own_group = lax.axis_index("seq") // group_size

    def valid_for(source):
        return lax.dynamic_slice_in_dim(key_valid, source * group_size, group_size, 0).reshape(-1)

    query_count = group_size * image_rows
    initial = (
        jnp.full((query_count, head_count), -jnp.inf, jnp.float32),
        jnp.zeros((query_count, head_count), jnp.float32),
        jnp.zeros((query_count, head_count, HEAD_DIM), jnp.float32),
    )
    carried = absorb(initial, key_value, valid_for(own_group), queries, head_count)

    def one_turn(turn_index, loop_state):
        current, moving = loop_state
        moving = shifted(moving, "seq", group_size)
        source = (own_group - turn_index) % group_count
        return (absorb(current, moving, valid_for(source), queries, head_count), moving)

    carried, key_value = lax.fori_loop(1, group_count, one_turn, (carried, key_value))
    running, denominator, numerator = carried
    attended = (numerator / denominator[:, :, None]).astype(jnp.bfloat16).reshape(query_count, -1)
    attended = ungroup(attended, bit_count)
    got_prev, got_next = pass_strips(attended.reshape(ROWS_DEV, WCOLS, -1))
    projected = project_rows(attended, w_out)
    from_prev = project_rows(got_prev, w_out)
    from_next = project_rows(got_next, w_out)
    weight_own = blend[0].reshape(ROWS_DEV, WCOLS, 1).astype(jnp.float32)
    partner = jnp.concatenate([from_prev, from_next], axis=1).astype(jnp.float32)
    joined = (
        weight_own * projected.astype(jnp.float32) + (blend_total - weight_own) * partner
    ) / blend_total
    return joined.astype(jnp.bfloat16).reshape(1, -1, joined.shape[-1])


MESH = pl.DeviceIdType.MESH
LOG2E = 1.4426950408889634


def partner_of(position, mask):
    bit = 1
    while bit <= mask:
        if mask & bit:
            position = position + (1 - 2 * ((position // bit) % 2)) * bit
        bit *= 2
    return position


def attend_kernel(
    count, rounds, query, key_image, key_text, value_image, value_text, prompt_ids, blend,
    out, queries, keys, values, left, right, prev_right, mixed, blends,
    send_sem, recv_sem, own_sem, blend_send, blend_recv, strip_send, strip_recv,
    back_send, back_recv, back_own, pass_send, pass_recv,
):
    image_rows = query.shape[1]
    text_rows = key_text.shape[1]
    all_image = count * image_rows
    strip_rows = image_rows // WCOLS
    pad_rows = keys.shape[1] - all_image - count * text_rows
    me = lax.axis_index("seq")
    windows = lax.axis_size("win")
    window = lax.axis_index("win")
    after = lax.rem(window + 1, windows)
    before = lax.rem(window + windows - 1, windows)
    masks = list(range(count - 1, 0, -1))

    barrier = pltpu.get_barrier_semaphore()
    for mask in masks:
        pl.semaphore_signal(barrier, inc=1, device_id={"seq": partner_of(me, mask)}, device_id_type=MESH)
    for other in (after, before):
        pl.semaphore_signal(barrier, inc=1, device_id={"win": other}, device_id_type=MESH)

    blends[me] = jnp.broadcast_to(blend[...].astype(jnp.float32), (8, image_rows))
    if pad_rows:
        zeros = jnp.zeros((rounds, pad_rows, HEAD_DIM), keys.dtype)
        keys[:, all_image + count * text_rows :, :] = zeros
        values[:, all_image + count * text_rows :, :] = zeros

    def pieces(turn, head, place):
        columns = pl.ds(pl.multiple_of(head * HEAD_DIM, HEAD_DIM), HEAD_DIM)
        image = pl.ds(pl.multiple_of(place * image_rows, image_rows), image_rows)
        text = pl.ds(pl.multiple_of(all_image + place * text_rows, text_rows), text_rows)
        return (
            (query.at[0, :, columns], queries.at[turn, image, :]),
            (key_image.at[0, :, columns], keys.at[turn, image, :]),
            (key_text.at[0, :, columns], keys.at[turn, text, :]),
            (value_image.at[0, :, columns], values.at[turn, image, :]),
            (value_text.at[0, :, columns], values.at[turn, text, :]),
        )

    def sends(turn, place_of=None):
        made = []
        for mask in masks:
            other = partner_of(me, mask)
            place = me if place_of is None else other
            for index, (source, target) in enumerate(pieces(turn, turn * count + other, place)):
                made.append(pltpu.make_async_remote_copy(
                    source, target, send_sem.at[turn, mask - 1, index], recv_sem.at[turn, mask - 1, index],
                    device_id={"seq": other}, device_id_type=MESH))
        return made

    def owns(turn):
        return [
            pltpu.make_async_copy(source, target, own_sem.at[turn, index])
            for index, (source, target) in enumerate(pieces(turn, turn * count + me, me))
        ]

    def blend_copies(place_of=None):
        made = []
        for mask in masks:
            other = partner_of(me, mask)
            place = me if place_of is None else other
            made.append(pltpu.make_async_remote_copy(
                blends.at[place], blends.at[place], blend_send.at[mask - 1], blend_recv.at[mask - 1],
                device_id={"seq": other}, device_id_type=MESH))
        return made

    def strip_copy(turn):
        return pltpu.make_async_remote_copy(
            right.at[turn], prev_right.at[turn], strip_send.at[turn], strip_recv.at[turn],
            device_id={"win": after}, device_id_type=MESH)

    def back_columns(turn, place):
        return pl.ds(pl.multiple_of((turn * count + place) * HEAD_DIM, HEAD_DIM), HEAD_DIM)

    def back_copies(turn, place_of=None):
        made = []
        for mask in masks:
            other = partner_of(me, mask)
            place = me if place_of is None else other
            made.append(pltpu.make_async_remote_copy(
                mixed.at[turn, pl.ds(other * strip_rows, strip_rows)],
                out.at[:, 0, :, back_columns(turn, place)],
                back_send.at[turn, mask - 1], back_recv.at[turn, mask - 1],
                device_id={"seq": other}, device_id_type=MESH))
        return made

    def back_local(turn):
        return pltpu.make_async_copy(
            mixed.at[turn, pl.ds(me * strip_rows, strip_rows)],
            out.at[:, 0, :, back_columns(turn, me)], back_own.at[turn])

    def pass_copy(turn):
        width = count * HEAD_DIM
        columns = pl.ds(pl.multiple_of(turn * width, width), width)
        return pltpu.make_async_remote_copy(
            out.at[:, 0, :, columns], out.at[:, 1, :, columns], pass_send.at[turn], pass_recv.at[turn],
            device_id={"win": before}, device_id_type=MESH)

    for turn in range(rounds):
        for copy in owns(turn):
            copy.start()
    pl.semaphore_wait(barrier, len(masks) + 2)
    for copy in blend_copies():
        copy.start()
    for turn in range(min(2, rounds)):
        for copy in sends(turn):
            copy.start()

    text_width = keys.shape[1] - all_image
    given = jnp.where(prompt_ids[...] != 0, 0.0, -jnp.inf).astype(jnp.float32)
    if pad_rows:
        given = jnp.concatenate([given, jnp.full((1, pad_rows), -jnp.inf, jnp.float32)], axis=1)
    scale = HEAD_DIM ** -0.5 * LOG2E
    token = lax.broadcasted_iota(jnp.int32, (strip_rows * STRIDE, image_rows), 1)
    spot = lax.broadcasted_iota(jnp.int32, (strip_rows * STRIDE, image_rows), 0)
    chosen = token == (spot // STRIDE) * WCOLS + spot % STRIDE
    contract = (((1,), (1,)), ((), ()))

    def one_round(turn, carry):
        for copy in sends(turn, 1):
            copy.wait_recv()
        for copy in owns(turn):
            copy.wait()

        def one_block(block, carry):
            rows = pl.ds(pl.multiple_of(block * image_rows, image_rows), image_rows)
            held = queries[turn, rows, :]
            image_scores = lax.dot_general(held, keys[turn, :all_image, :], contract, preferred_element_type=jnp.float32)
            text_scores = lax.dot_general(held, keys[turn, all_image:, :], contract, preferred_element_type=jnp.float32) + given
            peak = jnp.maximum(jnp.max(image_scores, axis=1, keepdims=True), jnp.max(text_scores, axis=1, keepdims=True))
            image_weights = jnp.exp2((image_scores - peak) * scale)
            text_weights = jnp.exp2((text_scores - peak) * scale)
            total = jnp.sum(image_weights, axis=1, keepdims=True) + jnp.sum(text_weights, axis=1, keepdims=True)
            product = jnp.dot(image_weights.astype(jnp.bfloat16), values[turn, :all_image, :], preferred_element_type=jnp.float32)
            product += jnp.dot(text_weights.astype(jnp.bfloat16), values[turn, all_image:, :], preferred_element_type=jnp.float32)
            attended = (product * (1.0 / total)).astype(jnp.bfloat16).reshape(strip_rows, WCOLS, HEAD_DIM)
            window_rows = pl.ds(block * strip_rows, strip_rows)
            left[turn, window_rows] = attended[:, :STRIDE]
            right[turn, window_rows] = attended[:, STRIDE:]
            return carry

        lax.fori_loop(0, count, one_block, 0)
        strip_copy(turn).start()

        @pl.when(turn == 0)
        def _():
            for copy in blend_copies(1):
                copy.wait_recv()

        strip_copy(turn).wait_recv()

        def one_mix(block, carry):
            window_rows = pl.ds(block * strip_rows, strip_rows)
            spread = jnp.where(chosen, blends[block][:1, :], 0.0).astype(jnp.bfloat16)
            own = jnp.dot(spread, jnp.ones((image_rows, HEAD_DIM), jnp.bfloat16), preferred_element_type=jnp.float32)
            own = own.reshape(strip_rows, STRIDE, HEAD_DIM)
            mine = left[turn, window_rows].astype(jnp.float32)
            theirs = prev_right[turn, window_rows].astype(jnp.float32)
            mixed[turn, window_rows] = ((own * mine + (blend_total - own) * theirs) * (1.0 / blend_total)).astype(jnp.bfloat16)
            return carry

        lax.fori_loop(0, count, one_mix, 0)
        for copy in back_copies(turn):
            copy.start()
        back_local(turn).start()

        @pl.when(turn + 2 < rounds)
        def _():
            for copy in sends(turn + 2):
                copy.start()

        return carry

    lax.fori_loop(0, rounds, one_round, 0)

    def one_pass(turn, carry):
        for copy in back_copies(turn, 1):
            copy.wait_recv()
        back_local(turn).wait()
        pass_copy(turn).start()
        return carry

    lax.fori_loop(0, rounds, one_pass, 0)

    def finish(turn, carry):
        for copy in sends(turn) + back_copies(turn):
            copy.wait_send()
        strip_copy(turn).wait_send()
        pass_copy(turn).wait()
        return carry

    lax.fori_loop(0, rounds, finish, 0)
    for copy in blend_copies():
        copy.wait_send()


def attend_in_kernel(count, query, key_image, value_image, key_text, value_text, prompt_ids, blend):
    image_rows, text_rows = query.shape[1], key_text.shape[1]
    rounds = query.shape[2] // HEAD_DIM // count
    all_image = count * image_rows
    key_rows = all_image + -(-count * text_rows // 128) * 128
    strip_rows = image_rows // WCOLS
    window_strip = (rounds, count * strip_rows, STRIDE, HEAD_DIM)
    anywhere = pl.BlockSpec(memory_space=pl.ANY)
    vmem = pl.BlockSpec(memory_space=pltpu.VMEM)
    dma = pltpu.SemaphoreType.DMA
    out = pl.pallas_call(
        functools.partial(attend_kernel, count, rounds),
        out_shape=jax.ShapeDtypeStruct((strip_rows, 2, STRIDE, query.shape[2]), jnp.bfloat16),
        in_specs=[anywhere] * 5 + [vmem] * 2,
        out_specs=anywhere,
        scratch_shapes=[
            pltpu.VMEM((rounds, all_image, HEAD_DIM), jnp.bfloat16),
            pltpu.VMEM((rounds, key_rows, HEAD_DIM), jnp.bfloat16),
            pltpu.VMEM((rounds, key_rows, HEAD_DIM), jnp.bfloat16),
            pltpu.VMEM(window_strip, jnp.bfloat16),
            pltpu.VMEM(window_strip, jnp.bfloat16),
            pltpu.VMEM(window_strip, jnp.bfloat16),
            pltpu.VMEM(window_strip, jnp.bfloat16),
            pltpu.VMEM((count, 8, image_rows), jnp.float32),
            dma((rounds, count - 1, 5)),
            dma((rounds, count - 1, 5)),
            dma((rounds, 5)),
            dma((count - 1,)),
            dma((count - 1,)),
            dma((rounds,)),
            dma((rounds,)),
            dma((rounds, count - 1)),
            dma((rounds, count - 1)),
            dma((rounds,)),
            dma((rounds,)),
            dma((rounds,)),
        ],
        compiler_params=pltpu.CompilerParams(
            collective_id=0, has_side_effects=True, vmem_limit_bytes=32 * 1024 * 1024
        ),
    )(query, key_image, key_text, value_image, value_text, prompt_ids, blend)
    return out.reshape(image_rows, query.shape[2])


def on_device_by_heads(query, key_image, value_image, key_text, value_text, prompt_ids, blend, w_out):
    blended = attend_in_kernel(
        lax.axis_size("seq"), query, key_image, value_image, key_text, value_text, prompt_ids, blend
    )
    joined = jnp.dot(blended, w_out, preferred_element_type=jnp.float32).astype(jnp.bfloat16)
    return joined[None]


def solution(mesh):
    seq_count = mesh.shape["seq"]
    by_heads = seq_count > 1 and seq_count & (seq_count - 1) == 0 and HEADS % seq_count == 0
    placed = (
        P(("pano", "win"), "seq", None),
        P(("pano", "win"), "seq", None),
        P(("pano", "win"), "seq", None),
        P(("pano", "win"), "seq", None),
        P(("pano", "win"), "seq", None),
        P(("pano", "win"), None),
        P(("pano", "win"), "seq"),
        P(),
    )
    return jax.shard_map(
        on_device_by_heads if by_heads else on_device,
        mesh=mesh,
        in_specs=placed,
        out_specs=P(("pano", "win"), "seq", None),
        check_vma=False,
    )
```

```python
import functools

import jax
import jax.numpy as jnp
from jax import lax
from jax.experimental import pallas as pl
from jax.experimental.pallas import tpu as pltpu
from jax.sharding import PartitionSpec as P

HEADS = 12
HEAD_DIM = 128
WCOLS = 64
ROWS_DEV = 3
STRIDE = 32


blend_total = 16.0


def swapped(block, axis, stride):
    count = lax.axis_size(axis)
    route = []
    for low in range(count):
        high = low | 1 << stride
        if high != low and high < count:
            route += [(low, high), (high, low)]
    return lax.ppermute(block, axis, route)


def shifted(block, axis, distance):
    devices = range(lax.axis_size(axis))
    route = [((i - distance) % len(devices), i) for i in devices]
    return lax.ppermute(block, axis, route)


def regroup(stacked, bit_count):
    row_count = stacked.shape[0]
    carried = stacked.reshape(row_count, 1 << bit_count, -1)
    position = lax.axis_index("seq")
    for bit_index in range(bit_count):
        own_bit = position >> bit_index & 1
        paired = carried.reshape(carried.shape[0], carried.shape[1] // 2, 2, carried.shape[2])
        kept_half = lax.dynamic_index_in_dim(paired, own_bit, 2, keepdims=False)
        sent_half = lax.dynamic_index_in_dim(paired, 1 - own_bit, 2, keepdims=False)
        received = swapped(sent_half, "seq", bit_index)
        lower_half = jnp.where(own_bit == 0, kept_half, received)
        upper_half = jnp.where(own_bit == 0, received, kept_half)
        carried = jnp.concatenate([lower_half, upper_half], axis=0)
    return carried.reshape(carried.shape[0], -1)


def ungroup(attended, bit_count):
    carried = attended.reshape(attended.shape[0], 1, attended.shape[1])
    position = lax.axis_index("seq")
    for bit_index in reversed(range(bit_count)):
        own_bit = position >> bit_index & 1
        halves = carried.reshape(2, carried.shape[0] // 2, carried.shape[1], carried.shape[2])
        kept_half = lax.dynamic_index_in_dim(halves, own_bit, 0, keepdims=False)
        sent_half = lax.dynamic_index_in_dim(halves, 1 - own_bit, 0, keepdims=False)
        received = swapped(sent_half, "seq", bit_index)
        lower_half = jnp.where(own_bit == 0, kept_half, received)
        upper_half = jnp.where(own_bit == 0, received, kept_half)
        stacked = jnp.stack([lower_half, upper_half], axis=2)
        carried = stacked.reshape(kept_half.shape[0], -1, kept_half.shape[2])
    return carried.reshape(carried.shape[0], -1)


def absorb(carried, key_value, valid_keys, queries, head_count):
    running, denominator, numerator = carried
    keys_block = key_value[0].reshape(key_value.shape[1], head_count, HEAD_DIM)
    values_block = key_value[1].reshape(key_value.shape[1], head_count, HEAD_DIM)
    scores = jnp.einsum(
        "qhd,khd->qhk", queries, keys_block, preferred_element_type=jnp.float32
    ) * HEAD_DIM ** (-0.5)
    scores = jnp.where(valid_keys[None, None, :], scores, -jnp.inf)
    updated = jnp.maximum(running, jnp.max(scores, axis=2))
    rescale = jnp.exp(running - updated)
    weights = jnp.exp(scores - updated[:, :, None])
    denominator = denominator * rescale + jnp.sum(weights, axis=2)
    product = jnp.einsum(
        "qhk,khd->qhd",
        weights.astype(jnp.bfloat16),
        values_block,
        preferred_element_type=jnp.float32,
    )
    numerator = numerator * rescale[:, :, None] + product
    return (updated, denominator, numerator)


def pass_strips(window_rows):
    from_prev = shifted(window_rows[:, STRIDE:], "win", 1)
    from_next = shifted(window_rows[:, :STRIDE], "win", -1)
    return (from_prev, from_next)


def project_rows(features, w_out):
    flat_rows = features.reshape(-1, features.shape[-1])
    result = jnp.dot(flat_rows, w_out, preferred_element_type=jnp.float32).astype(jnp.bfloat16)
    return result.reshape(ROWS_DEV, -1, w_out.shape[1])


def on_device(query, key_image, value_image, key_text, value_text, prompt_ids, blend, w_out):
    bit_count = 2
    group_size = 1 << bit_count
    image_rows = query.shape[1]
    text_rows = key_text.shape[1]
    key_rows = image_rows + text_rows
    head_count = HEADS // group_size
    stacked = jnp.concatenate(
        [query[0], key_image[0], key_text[0], value_image[0], value_text[0]], axis=0
    )
    grouped = regroup(stacked, bit_count).reshape(group_size, image_rows + 2 * key_rows, -1)
    queries = grouped[:, :image_rows].reshape(group_size * image_rows, head_count, HEAD_DIM)
    keys_grouped = grouped[:, image_rows : image_rows + key_rows].reshape(group_size * key_rows, -1)
    values_grouped = grouped[:, image_rows + key_rows :].reshape(group_size * key_rows, -1)
    key_value = jnp.stack([keys_grouped, values_grouped])
    seq_count = lax.axis_size("seq")
    text_valid = prompt_ids[0].reshape(seq_count, text_rows) != 0
    key_valid = jnp.concatenate([jnp.ones((seq_count, image_rows), jnp.bool_), text_valid], axis=1)
    group_count = seq_count // group_size
    own_group = lax.axis_index("seq") // group_size

    def valid_for(source):
        return lax.dynamic_slice_in_dim(key_valid, source * group_size, group_size, 0).reshape(-1)

    query_count = group_size * image_rows
    initial = (
        jnp.full((query_count, head_count), -jnp.inf, jnp.float32),
        jnp.zeros((query_count, head_count), jnp.float32),
        jnp.zeros((query_count, head_count, HEAD_DIM), jnp.float32),
    )
    carried = absorb(initial, key_value, valid_for(own_group), queries, head_count)

    def one_turn(turn_index, loop_state):
        current, moving = loop_state
        moving = shifted(moving, "seq", group_size)
        source = (own_group - turn_index) % group_count
        return (absorb(current, moving, valid_for(source), queries, head_count), moving)

    carried, key_value = lax.fori_loop(1, group_count, one_turn, (carried, key_value))
    running, denominator, numerator = carried
    attended = (numerator / denominator[:, :, None]).astype(jnp.bfloat16).reshape(query_count, -1)
    attended = ungroup(attended, bit_count)
    got_prev, got_next = pass_strips(attended.reshape(ROWS_DEV, WCOLS, -1))
    projected = project_rows(attended, w_out)
    from_prev = project_rows(got_prev, w_out)
    from_next = project_rows(got_next, w_out)
    weight_own = blend[0].reshape(ROWS_DEV, WCOLS, 1).astype(jnp.float32)
    partner = jnp.concatenate([from_prev, from_next], axis=1).astype(jnp.float32)
    joined = (
        weight_own * projected.astype(jnp.float32) + (blend_total - weight_own) * partner
    ) / blend_total
    return joined.astype(jnp.bfloat16).reshape(1, -1, joined.shape[-1])


MESH = pl.DeviceIdType.MESH
LOG2E = 1.4426950408889634


VMEM_GRANT = 60 * 1024 * 1024


def partner_of(position, mask):
    bit = 1
    while bit <= mask:
        if mask & bit:
            position = position + (1 - 2 * ((position // bit) % 2)) * bit
        bit *= 2
    return position


def window_kernel(
    count, rounds, query, key_image, key_text, value_image, value_text, prompt_ids, blend, w_out,
    out, queries, keys, values, left, right, prev_right, mixed, blends, features, weights, partial,
    send_sem, recv_sem, own_sem, blend_send, blend_recv, strip_send, strip_recv,
    back_send, back_recv, back_own, pass_send, pass_recv, weight_sem,
):
    image_rows = query.shape[1]
    text_rows = key_text.shape[1]
    all_image = count * image_rows
    strip_rows = image_rows // WCOLS
    strip_size = strip_rows * STRIDE
    pad_rows = keys.shape[1] - all_image - count * text_rows
    width = count * HEAD_DIM
    me = lax.axis_index("seq")
    windows = lax.axis_size("win")
    window = lax.axis_index("win")
    after = lax.rem(window + 1, windows)
    before = lax.rem(window + windows - 1, windows)
    masks = list(range(count - 1, 0, -1))

    barrier = pltpu.get_barrier_semaphore()
    for mask in masks:
        pl.semaphore_signal(barrier, inc=1, device_id={"seq": partner_of(me, mask)}, device_id_type=MESH)
    for other in (after, before):
        pl.semaphore_signal(barrier, inc=1, device_id={"win": other}, device_id_type=MESH)

    def pieces(turn, head, place):
        columns = pl.ds(pl.multiple_of(head * HEAD_DIM, HEAD_DIM), HEAD_DIM)
        image = pl.ds(pl.multiple_of(place * image_rows, image_rows), image_rows)
        text = pl.ds(pl.multiple_of(all_image + place * text_rows, text_rows), text_rows)
        return (
            (key_image.at[0, :, columns], keys.at[turn, image, :]),
            (key_text.at[0, :, columns], keys.at[turn, text, :]),
            (value_image.at[0, :, columns], values.at[turn, image, :]),
            (value_text.at[0, :, columns], values.at[turn, text, :]),
            (query.at[0, :, columns], queries.at[turn, image, :]),
        )

    def moves(turn, mask, arriving=False, indices=range(5)):
        other = partner_of(me, mask)
        made = pieces(turn, turn * count + other, other if arriving else me)
        if mask == 0:
            return [pltpu.make_async_copy(s, t, own_sem.at[turn, i]) for i, (s, t) in enumerate(made) if i in indices]
        return [
            pltpu.make_async_remote_copy(
                s, t, send_sem.at[turn, mask - 1, i], recv_sem.at[turn, mask - 1, i],
                device_id={"seq": other}, device_id_type=MESH)
            for i, (s, t) in enumerate(made)
            if i in indices
        ]

    def send_keys(turn):
        for index in range(4):
            for mask in masks:
                moves(turn, mask, indices=[index])[0].start()

    def send_queries(turn):
        for mask in masks:
            moves(turn, mask, indices=[4])[0].start()

    def arrived(turn, mask, indices):
        for copy in moves(turn, mask, True, indices):
            if mask == 0:
                copy.wait()
            else:
                copy.wait_recv()

    def blend_copy(mask, arriving=False):
        other = partner_of(me, mask)
        place = other if arriving else me
        return pltpu.make_async_remote_copy(
            blends.at[place], blends.at[place], blend_send.at[mask - 1], blend_recv.at[mask - 1],
            device_id={"seq": other}, device_id_type=MESH)

    def strip_place(mask):
        place = partner_of(me, mask)
        return pl.ds(pl.multiple_of(place * strip_size, strip_size), strip_size)

    def strip_copy(turn, mask):
        rows = strip_place(mask)
        return pltpu.make_async_remote_copy(
            right.at[turn, rows], prev_right.at[turn, rows], strip_send.at[turn, mask], strip_recv.at[turn, mask],
            device_id={"win": after}, device_id_type=MESH)

    def head_columns(turn, place):
        return pl.ds(pl.multiple_of((turn * count + place) * HEAD_DIM, HEAD_DIM), HEAD_DIM)

    def back_copy(turn, mask, arriving=False):
        other = partner_of(me, mask)
        source = mixed.at[turn, strip_place(mask)]
        target = features.at[0, :, head_columns(turn, other if arriving else me)]
        if mask == 0:
            return pltpu.make_async_copy(source, target, back_own.at[turn])
        return pltpu.make_async_remote_copy(
            source, target, back_send.at[turn, mask - 1], back_recv.at[turn, mask - 1],
            device_id={"seq": other}, device_id_type=MESH)

    def pass_copy(turn, mask):
        columns = head_columns(turn, partner_of(me, mask))
        return pltpu.make_async_remote_copy(
            features.at[0, :, columns], features.at[1, :, columns], pass_send.at[turn, mask], pass_recv.at[turn, mask],
            device_id={"win": before}, device_id_type=MESH)

    def weight_copy(turn):
        rows = pl.ds(turn * width, width)
        return pltpu.make_async_copy(w_out.at[rows, :], weights.at[rows, :], weight_sem.at[turn])

    blends[me] = jnp.broadcast_to(blend[...].astype(jnp.float32), (8, image_rows))
    pl.semaphore_wait(barrier, len(masks) + 2)
    for turn in range(min(2, rounds)):
        send_keys(turn)
        send_queries(turn)
        if turn == 0:
            for mask in masks:
                blend_copy(mask).start()
    for turn in range(rounds):
        for copy in moves(turn, 0):
            copy.start()
    for turn in range(rounds):
        weight_copy(turn).start()

    if pad_rows:
        zeros = jnp.zeros((rounds, pad_rows, HEAD_DIM), keys.dtype)
        keys[:, all_image + count * text_rows :, :] = zeros
        values[:, all_image + count * text_rows :, :] = zeros
    given = jnp.where(prompt_ids[...] != 0, 0.0, -jnp.inf).astype(jnp.float32)
    if pad_rows:
        given = jnp.concatenate([given, jnp.full((1, pad_rows), -jnp.inf, jnp.float32)], axis=1)
    scale = HEAD_DIM ** -0.5 * LOG2E
    contract = (((1,), (1,)), ((), ()))

    def attend(turn, mask):
        place = partner_of(me, mask)
        held = queries[turn, pl.ds(pl.multiple_of(place * image_rows, image_rows), image_rows), :]
        image_scores = lax.dot_general(held, keys[turn, :all_image, :], contract, preferred_element_type=jnp.float32)
        text_scores = lax.dot_general(held, keys[turn, all_image:, :], contract, preferred_element_type=jnp.float32) + given
        peak = jnp.maximum(jnp.max(image_scores, axis=1, keepdims=True), jnp.max(text_scores, axis=1, keepdims=True))
        image_weights = jnp.exp2((image_scores - peak) * scale)
        text_weights = jnp.exp2((text_scores - peak) * scale)
        total = jnp.sum(image_weights, axis=1, keepdims=True) + jnp.sum(text_weights, axis=1, keepdims=True)
        product = jnp.dot(image_weights.astype(jnp.bfloat16), values[turn, :all_image, :], preferred_element_type=jnp.float32)
        product += jnp.dot(text_weights.astype(jnp.bfloat16), values[turn, all_image:, :], preferred_element_type=jnp.float32)
        attended = (product * (1.0 / total)).astype(jnp.bfloat16).reshape(strip_rows, WCOLS, HEAD_DIM)
        left[turn, strip_place(mask), :] = attended[:, :STRIDE].reshape(strip_size, HEAD_DIM)
        right[turn, strip_place(mask), :] = attended[:, STRIDE:].reshape(strip_size, HEAD_DIM)

    def own_weight(mask):
        token = lax.broadcasted_iota(jnp.int32, (strip_size, image_rows), 1)
        spot = lax.broadcasted_iota(jnp.int32, (strip_size, image_rows), 0)
        chosen = token == (spot // STRIDE) * WCOLS + spot % STRIDE
        spread = jnp.where(chosen, blends[partner_of(me, mask)][:1, :], 0.0).astype(jnp.bfloat16)
        return jnp.dot(spread, jnp.ones((image_rows, HEAD_DIM), jnp.bfloat16), preferred_element_type=jnp.float32)

    def mix(turn, mask):
        if turn == 0 and mask != 0:
            blend_copy(mask, True).wait_recv()
        strip_copy(turn, mask).wait_recv()
        own = own_weight(mask)
        mine = left[turn, strip_place(mask), :].astype(jnp.float32)
        theirs = prev_right[turn, strip_place(mask), :].astype(jnp.float32)
        mixed[turn, strip_place(mask), :] = ((own * mine + (blend_total - own) * theirs) * (1.0 / blend_total)).astype(jnp.bfloat16)
        back_copy(turn, mask).start()

    def pass_on(turn, order):
        for mask in order:
            copy = back_copy(turn, mask, True)
            if mask == 0:
                copy.wait()
            else:
                copy.wait_recv()
            pass_copy(turn, mask).start()

    tile = 512

    def project(turn, halves):
        first, final = turn == 0, turn == rounds - 1
        low, high = halves[0] * strip_size, (halves[-1] + 1) * strip_size
        rows = features[halves[0] : halves[-1] + 1, :, turn * width : (turn + 1) * width].reshape(high - low, width)

        def one_tile(index, carry):
            columns = pl.ds(pl.multiple_of(index * tile, tile), tile)
            result = jnp.dot(rows, weights[turn * width : (turn + 1) * width, columns], preferred_element_type=jnp.float32)
            if not first:
                result = result + partial[low:high, columns]
            if not final:
                partial[low:high, columns] = result
            else:
                result = result.astype(jnp.bfloat16).reshape(len(halves), strip_rows, STRIDE, tile)
                for place, half in enumerate(halves):
                    out[:, half, :, columns] = result[place]
            return carry

        lax.fori_loop(0, weights.shape[1] // tile, one_tile, 0)

    blocks = masks + [0]
    for turn in range(rounds):
        final = turn == rounds - 1
        if final:
            pass_on(turn - 1, blocks)
        for mask in blocks:
            arrived(turn, mask, range(4))
        lag = 2
        for step in range(len(blocks) + lag):
            if step < len(blocks):
                arrived(turn, blocks[step], [4])
                attend(turn, blocks[step])
                strip_copy(turn, blocks[step]).start()
            if step >= lag:
                mix(turn, blocks[step - lag])
        if 2 <= turn + 1 < rounds:
            send_queries(turn + 1)
        if turn + 2 < rounds:
            send_keys(turn + 2)
        if turn >= 1 and not final:
            pass_on(turn - 1, blocks)
            if turn == 1:
                for other in range(rounds):
                    weight_copy(other).wait()
            for mask in blocks:
                pass_copy(turn - 1, mask).wait_recv()
            project(turn - 1, (0, 1))

    final = rounds - 1
    pass_on(final, [0])
    for mask in blocks:
        pass_copy(final - 1, mask).wait_recv()
    project(final - 1, (0, 1))
    pass_on(final, masks[::-1])
    project(final, (0,))
    for mask in blocks:
        pass_copy(final, mask).wait_recv()
    project(final, (1,))

    for turn in range(rounds):
        for mask in blocks:
            strip_copy(turn, mask).wait_send()
            pass_copy(turn, mask).wait_send()
            if mask != 0:
                back_copy(turn, mask).wait_send()
                for copy in moves(turn, mask):
                    copy.wait_send()
    for mask in masks:
        blend_copy(mask).wait_send()


def on_device_by_heads(query, key_image, value_image, key_text, value_text, prompt_ids, blend, w_out):
    count = lax.axis_size("seq")
    image_rows, text_rows = query.shape[1], key_text.shape[1]
    rounds = query.shape[2] // HEAD_DIM // count
    all_image = count * image_rows
    key_rows = all_image + -(-count * text_rows // 128) * 128
    strip_rows = image_rows // WCOLS
    window_strip = (rounds, count * strip_rows * STRIDE, HEAD_DIM)
    anywhere = pl.BlockSpec(memory_space=pl.ANY)
    vmem = pl.BlockSpec(memory_space=pltpu.VMEM)
    dma = pltpu.SemaphoreType.DMA
    out = pl.pallas_call(
        functools.partial(window_kernel, count, rounds),
        out_shape=jax.ShapeDtypeStruct((strip_rows, 2, STRIDE, w_out.shape[1]), jnp.bfloat16),
        in_specs=[anywhere] * 5 + [vmem] * 2 + [anywhere],
        out_specs=vmem,
        scratch_shapes=[
            pltpu.VMEM((rounds, all_image, HEAD_DIM), jnp.bfloat16),
            pltpu.VMEM((rounds, key_rows, HEAD_DIM), jnp.bfloat16),
            pltpu.VMEM((rounds, key_rows, HEAD_DIM), jnp.bfloat16),
            pltpu.VMEM(window_strip, jnp.bfloat16),
            pltpu.VMEM(window_strip, jnp.bfloat16),
            pltpu.VMEM(window_strip, jnp.bfloat16),
            pltpu.VMEM(window_strip, jnp.bfloat16),
            pltpu.VMEM((count, 8, image_rows), jnp.float32),
            pltpu.VMEM((2, strip_rows * STRIDE, query.shape[2]), jnp.bfloat16),
            pltpu.VMEM(w_out.shape, jnp.bfloat16),
            pltpu.VMEM((image_rows, w_out.shape[1]), jnp.float32),
            dma((rounds, count - 1, 5)),
            dma((rounds, count - 1, 5)),
            dma((rounds, 5)),
            dma((count - 1,)),
            dma((count - 1,)),
            dma((rounds, count)),
            dma((rounds, count)),
            dma((rounds, count - 1)),
            dma((rounds, count - 1)),
            dma((rounds,)),
            dma((rounds, count)),
            dma((rounds, count)),
            dma((rounds,)),
        ],
        compiler_params=pltpu.CompilerParams(
            collective_id=0, has_side_effects=True, vmem_limit_bytes=VMEM_GRANT
        ),
    )(query, key_image, key_text, value_image, value_text, prompt_ids, blend, w_out)
    return out.reshape(1, image_rows, w_out.shape[1])


def solution(mesh):
    seq_count = mesh.shape["seq"]
    by_heads = seq_count > 1 and seq_count & (seq_count - 1) == 0 and HEADS % seq_count == 0
    placed = (
        P(("pano", "win"), "seq", None),
        P(("pano", "win"), "seq", None),
        P(("pano", "win"), "seq", None),
        P(("pano", "win"), "seq", None),
        P(("pano", "win"), "seq", None),
        P(("pano", "win"), None),
        P(("pano", "win"), "seq"),
        P(),
    )
    return jax.shard_map(
        on_device_by_heads if by_heads else on_device,
        mesh=mesh,
        in_specs=placed,
        out_specs=P(("pano", "win"), "seq", None),
        check_vma=False,
    )
```

```python
import functools

import jax
import jax.numpy as jnp
from jax import lax
from jax.experimental import pallas as pl
from jax.experimental.pallas import tpu as pltpu
from jax.sharding import PartitionSpec as P

HEADS = 12
HEAD_DIM = 128
WCOLS = 64
ROWS_DEV = 3
STRIDE = 32


blend_total = 16.0


def swapped(block, axis, stride):
    count = lax.axis_size(axis)
    route = []
    for low in range(count):
        high = low | 1 << stride
        if high != low and high < count:
            route += [(low, high), (high, low)]
    return lax.ppermute(block, axis, route)


def shifted(block, axis, distance):
    devices = range(lax.axis_size(axis))
    route = [((i - distance) % len(devices), i) for i in devices]
    return lax.ppermute(block, axis, route)


def regroup(stacked, bit_count):
    row_count = stacked.shape[0]
    carried = stacked.reshape(row_count, 1 << bit_count, -1)
    position = lax.axis_index("seq")
    for bit_index in range(bit_count):
        own_bit = position >> bit_index & 1
        paired = carried.reshape(carried.shape[0], carried.shape[1] // 2, 2, carried.shape[2])
        kept_half = lax.dynamic_index_in_dim(paired, own_bit, 2, keepdims=False)
        sent_half = lax.dynamic_index_in_dim(paired, 1 - own_bit, 2, keepdims=False)
        received = swapped(sent_half, "seq", bit_index)
        lower_half = jnp.where(own_bit == 0, kept_half, received)
        upper_half = jnp.where(own_bit == 0, received, kept_half)
        carried = jnp.concatenate([lower_half, upper_half], axis=0)
    return carried.reshape(carried.shape[0], -1)


def ungroup(attended, bit_count):
    carried = attended.reshape(attended.shape[0], 1, attended.shape[1])
    position = lax.axis_index("seq")
    for bit_index in reversed(range(bit_count)):
        own_bit = position >> bit_index & 1
        halves = carried.reshape(2, carried.shape[0] // 2, carried.shape[1], carried.shape[2])
        kept_half = lax.dynamic_index_in_dim(halves, own_bit, 0, keepdims=False)
        sent_half = lax.dynamic_index_in_dim(halves, 1 - own_bit, 0, keepdims=False)
        received = swapped(sent_half, "seq", bit_index)
        lower_half = jnp.where(own_bit == 0, kept_half, received)
        upper_half = jnp.where(own_bit == 0, received, kept_half)
        stacked = jnp.stack([lower_half, upper_half], axis=2)
        carried = stacked.reshape(kept_half.shape[0], -1, kept_half.shape[2])
    return carried.reshape(carried.shape[0], -1)


def absorb(carried, key_value, valid_keys, queries, head_count):
    running, denominator, numerator = carried
    keys_block = key_value[0].reshape(key_value.shape[1], head_count, HEAD_DIM)
    values_block = key_value[1].reshape(key_value.shape[1], head_count, HEAD_DIM)
    scores = jnp.einsum(
        "qhd,khd->qhk", queries, keys_block, preferred_element_type=jnp.float32
    ) * HEAD_DIM ** (-0.5)
    scores = jnp.where(valid_keys[None, None, :], scores, -jnp.inf)
    updated = jnp.maximum(running, jnp.max(scores, axis=2))
    rescale = jnp.exp(running - updated)
    weights = jnp.exp(scores - updated[:, :, None])
    denominator = denominator * rescale + jnp.sum(weights, axis=2)
    product = jnp.einsum(
        "qhk,khd->qhd",
        weights.astype(jnp.bfloat16),
        values_block,
        preferred_element_type=jnp.float32,
    )
    numerator = numerator * rescale[:, :, None] + product
    return (updated, denominator, numerator)


def pass_strips(window_rows):
    from_prev = shifted(window_rows[:, STRIDE:], "win", 1)
    from_next = shifted(window_rows[:, :STRIDE], "win", -1)
    return (from_prev, from_next)


def project_rows(features, w_out):
    flat_rows = features.reshape(-1, features.shape[-1])
    result = jnp.dot(flat_rows, w_out, preferred_element_type=jnp.float32).astype(jnp.bfloat16)
    return result.reshape(ROWS_DEV, -1, w_out.shape[1])


def on_device(query, key_image, value_image, key_text, value_text, prompt_ids, blend, w_out):
    bit_count = 2
    group_size = 1 << bit_count
    image_rows = query.shape[1]
    text_rows = key_text.shape[1]
    key_rows = image_rows + text_rows
    head_count = HEADS // group_size
    stacked = jnp.concatenate(
        [query[0], key_image[0], key_text[0], value_image[0], value_text[0]], axis=0
    )
    grouped = regroup(stacked, bit_count).reshape(group_size, image_rows + 2 * key_rows, -1)
    queries = grouped[:, :image_rows].reshape(group_size * image_rows, head_count, HEAD_DIM)
    keys_grouped = grouped[:, image_rows : image_rows + key_rows].reshape(group_size * key_rows, -1)
    values_grouped = grouped[:, image_rows + key_rows :].reshape(group_size * key_rows, -1)
    key_value = jnp.stack([keys_grouped, values_grouped])
    seq_count = lax.axis_size("seq")
    text_valid = prompt_ids[0].reshape(seq_count, text_rows) != 0
    key_valid = jnp.concatenate([jnp.ones((seq_count, image_rows), jnp.bool_), text_valid], axis=1)
    group_count = seq_count // group_size
    own_group = lax.axis_index("seq") // group_size

    def valid_for(source):
        return lax.dynamic_slice_in_dim(key_valid, source * group_size, group_size, 0).reshape(-1)

    query_count = group_size * image_rows
    initial = (
        jnp.full((query_count, head_count), -jnp.inf, jnp.float32),
        jnp.zeros((query_count, head_count), jnp.float32),
        jnp.zeros((query_count, head_count, HEAD_DIM), jnp.float32),
    )
    carried = absorb(initial, key_value, valid_for(own_group), queries, head_count)

    def one_turn(turn_index, loop_state):
        current, moving = loop_state
        moving = shifted(moving, "seq", group_size)
        source = (own_group - turn_index) % group_count
        return (absorb(current, moving, valid_for(source), queries, head_count), moving)

    carried, key_value = lax.fori_loop(1, group_count, one_turn, (carried, key_value))
    running, denominator, numerator = carried
    attended = (numerator / denominator[:, :, None]).astype(jnp.bfloat16).reshape(query_count, -1)
    attended = ungroup(attended, bit_count)
    got_prev, got_next = pass_strips(attended.reshape(ROWS_DEV, WCOLS, -1))
    projected = project_rows(attended, w_out)
    from_prev = project_rows(got_prev, w_out)
    from_next = project_rows(got_next, w_out)
    weight_own = blend[0].reshape(ROWS_DEV, WCOLS, 1).astype(jnp.float32)
    partner = jnp.concatenate([from_prev, from_next], axis=1).astype(jnp.float32)
    joined = (
        weight_own * projected.astype(jnp.float32) + (blend_total - weight_own) * partner
    ) / blend_total
    return joined.astype(jnp.bfloat16).reshape(1, -1, joined.shape[-1])


MESH = pl.DeviceIdType.MESH
LOG2E = 1.4426950408889634


VMEM_GRANT = 28 * 1024 * 1024


def partner_of(position, mask):
    bit = 1
    while bit <= mask:
        if mask & bit:
            position = position + (1 - 2 * ((position // bit) % 2)) * bit
        bit *= 2
    return position


def window_kernel(
    count, rounds, query, key_image, key_text, value_image, value_text, prompt_ids, blend, w_out,
    out, queries, keys, values, left, right, prev_right, mixed, blends, features, weights, partial,
    send_sem, recv_sem, own_sem, blend_send, blend_recv, strip_send, strip_recv,
    back_send, back_recv, back_own, pass_send, pass_recv, weight_sem, ids_held, blend_held, small_sem,
):
    image_rows = query.shape[1]
    text_rows = key_text.shape[1]
    all_image = count * image_rows
    strip_rows = image_rows // WCOLS
    strip_size = strip_rows * STRIDE
    pad_rows = keys.shape[1] - all_image - count * text_rows
    width = count * HEAD_DIM
    me = lax.axis_index("seq")
    windows = lax.axis_size("win")
    window = lax.axis_index("win")
    after = lax.rem(window + 1, windows)
    before = lax.rem(window + windows - 1, windows)
    masks = list(range(count - 1, 0, -1))

    small = [
        pltpu.make_async_copy(prompt_ids, ids_held, small_sem.at[0]),
        pltpu.make_async_copy(blend, blend_held, small_sem.at[1]),
    ]
    for copy in small:
        copy.start()
    barrier = pltpu.get_barrier_semaphore()
    for mask in masks:
        pl.semaphore_signal(barrier, inc=1, device_id={"seq": partner_of(me, mask)}, device_id_type=MESH)
    for other in (after, before):
        pl.semaphore_signal(barrier, inc=1, device_id={"win": other}, device_id_type=MESH)

    def pieces(turn, head, place):
        columns = pl.ds(pl.multiple_of(head * HEAD_DIM, HEAD_DIM), HEAD_DIM)
        image = pl.ds(pl.multiple_of(place * image_rows, image_rows), image_rows)
        text = pl.ds(pl.multiple_of(all_image + place * text_rows, text_rows), text_rows)
        return (
            (key_image.at[0, :, columns], keys.at[turn, image, :]),
            (key_text.at[0, :, columns], keys.at[turn, text, :]),
            (value_image.at[0, :, columns], values.at[turn, image, :]),
            (value_text.at[0, :, columns], values.at[turn, text, :]),
            (query.at[0, :, columns], queries.at[turn, image, :]),
        )

    def moves(turn, mask, arriving=False, indices=range(5)):
        other = partner_of(me, mask)
        made = pieces(turn, turn * count + other, other if arriving else me)
        if mask == 0:
            return [pltpu.make_async_copy(s, t, own_sem.at[turn, i]) for i, (s, t) in enumerate(made) if i in indices]
        return [
            pltpu.make_async_remote_copy(
                s, t, send_sem.at[turn, mask - 1, i], recv_sem.at[turn, mask - 1, i],
                device_id={"seq": other}, device_id_type=MESH)
            for i, (s, t) in enumerate(made)
            if i in indices
        ]

    def send_keys(turn):
        for index in range(4):
            for mask in masks:
                moves(turn, mask, indices=[index])[0].start()

    def send_queries(turn):
        for mask in masks:
            moves(turn, mask, indices=[4])[0].start()

    def arrived(turn, mask, indices):
        for copy in moves(turn, mask, True, indices):
            if mask == 0:
                copy.wait()
            else:
                copy.wait_recv()

    def blend_copy(mask, arriving=False):
        other = partner_of(me, mask)
        place = other if arriving else me
        return pltpu.make_async_remote_copy(
            blends.at[place], blends.at[place], blend_send.at[mask - 1], blend_recv.at[mask - 1],
            device_id={"seq": other}, device_id_type=MESH)

    def strip_place(mask):
        place = partner_of(me, mask)
        return pl.ds(pl.multiple_of(place * strip_size, strip_size), strip_size)

    def strip_copy(turn, mask):
        rows = strip_place(mask)
        return pltpu.make_async_remote_copy(
            right.at[turn, rows], prev_right.at[turn, rows], strip_send.at[turn, mask], strip_recv.at[turn, mask],
            device_id={"win": after}, device_id_type=MESH)

    def head_columns(turn, place):
        return pl.ds(pl.multiple_of((turn * count + place) * HEAD_DIM, HEAD_DIM), HEAD_DIM)

    def back_copy(turn, mask, arriving=False):
        other = partner_of(me, mask)
        source = mixed.at[turn, strip_place(mask)]
        target = features.at[0, :, head_columns(turn, other if arriving else me)]
        if mask == 0:
            return pltpu.make_async_copy(source, target, back_own.at[turn])
        return pltpu.make_async_remote_copy(
            source, target, back_send.at[turn, mask - 1], back_recv.at[turn, mask - 1],
            device_id={"seq": other}, device_id_type=MESH)

    def pass_copy(turn, mask):
        columns = head_columns(turn, partner_of(me, mask))
        return pltpu.make_async_remote_copy(
            features.at[0, :, columns], features.at[1, :, columns], pass_send.at[turn, mask], pass_recv.at[turn, mask],
            device_id={"win": before}, device_id_type=MESH)

    def weight_copy(turn):
        rows = pl.ds(turn * width, width)
        return pltpu.make_async_copy(w_out.at[rows, :], weights.at[rows, :], weight_sem.at[turn])

    for copy in small:
        copy.wait()
    blends[me] = jnp.broadcast_to(blend_held[...].astype(jnp.float32), (8, image_rows))
    pl.semaphore_wait(barrier, len(masks) + 2)
    for turn in range(min(2, rounds)):
        send_keys(turn)
        send_queries(turn)
        if turn == 0:
            for mask in masks:
                blend_copy(mask).start()
    for turn in range(rounds):
        for copy in moves(turn, 0):
            copy.start()
    for turn in range(rounds):
        weight_copy(turn).start()

    if pad_rows:
        zeros = jnp.zeros((rounds, pad_rows, HEAD_DIM), keys.dtype)
        keys[:, all_image + count * text_rows :, :] = zeros
        values[:, all_image + count * text_rows :, :] = zeros
    given = jnp.where(ids_held[...] != 0, 0.0, -jnp.inf).astype(jnp.float32)
    if pad_rows:
        given = jnp.concatenate([given, jnp.full((1, pad_rows), -jnp.inf, jnp.float32)], axis=1)
    scale = HEAD_DIM ** -0.5 * LOG2E
    contract = (((1,), (1,)), ((), ()))

    def attend(turn, mask):
        place = partner_of(me, mask)
        held = queries[turn, pl.ds(pl.multiple_of(place * image_rows, image_rows), image_rows), :]
        image_scores = lax.dot_general(held, keys[turn, :all_image, :], contract, preferred_element_type=jnp.float32)
        text_scores = lax.dot_general(held, keys[turn, all_image:, :], contract, preferred_element_type=jnp.float32) + given
        peak = jnp.maximum(jnp.max(image_scores, axis=1, keepdims=True), jnp.max(text_scores, axis=1, keepdims=True))
        image_weights = jnp.exp2((image_scores - peak) * scale)
        text_weights = jnp.exp2((text_scores - peak) * scale)
        total = jnp.sum(image_weights, axis=1, keepdims=True) + jnp.sum(text_weights, axis=1, keepdims=True)
        product = jnp.dot(image_weights.astype(jnp.bfloat16), values[turn, :all_image, :], preferred_element_type=jnp.float32)
        product += jnp.dot(text_weights.astype(jnp.bfloat16), values[turn, all_image:, :], preferred_element_type=jnp.float32)
        attended = (product * (1.0 / total)).astype(jnp.bfloat16).reshape(strip_rows, WCOLS, HEAD_DIM)
        left[turn, strip_place(mask), :] = attended[:, :STRIDE].reshape(strip_size, HEAD_DIM)
        right[turn, strip_place(mask), :] = attended[:, STRIDE:].reshape(strip_size, HEAD_DIM)

    def own_weight(mask):
        token = lax.broadcasted_iota(jnp.int32, (strip_size, image_rows), 1)
        spot = lax.broadcasted_iota(jnp.int32, (strip_size, image_rows), 0)
        chosen = token == (spot // STRIDE) * WCOLS + spot % STRIDE
        spread = jnp.where(chosen, blends[partner_of(me, mask)][:1, :], 0.0).astype(jnp.bfloat16)
        return jnp.dot(spread, jnp.ones((image_rows, HEAD_DIM), jnp.bfloat16), preferred_element_type=jnp.float32)

    def mix(turn, mask):
        if turn == 0 and mask != 0:
            blend_copy(mask, True).wait_recv()
        strip_copy(turn, mask).wait_recv()
        own = own_weight(mask)
        mine = left[turn, strip_place(mask), :].astype(jnp.float32)
        theirs = prev_right[turn, strip_place(mask), :].astype(jnp.float32)
        mixed[turn, strip_place(mask), :] = ((own * mine + (blend_total - own) * theirs) * (1.0 / blend_total)).astype(jnp.bfloat16)
        back_copy(turn, mask).start()

    def pass_on(turn, order):
        for mask in order:
            copy = back_copy(turn, mask, True)
            if mask == 0:
                copy.wait()
            else:
                copy.wait_recv()
            pass_copy(turn, mask).start()

    tile = 512

    def project(turn, halves):
        first, final = turn == 0, turn == rounds - 1
        low, high = halves[0] * strip_size, (halves[-1] + 1) * strip_size
        rows = features[halves[0] : halves[-1] + 1, :, turn * width : (turn + 1) * width].reshape(high - low, width)

        def one_tile(index, carry):
            columns = pl.ds(pl.multiple_of(index * tile, tile), tile)
            result = jnp.dot(rows, weights[turn * width : (turn + 1) * width, columns], preferred_element_type=jnp.float32)
            if not first:
                result = result + partial[low:high, columns]
            if not final:
                partial[low:high, columns] = result
            else:
                result = result.astype(jnp.bfloat16).reshape(len(halves), strip_rows, STRIDE, tile)
                for place, half in enumerate(halves):
                    out[:, half, :, columns] = result[place]
            return carry

        lax.fori_loop(0, weights.shape[1] // tile, one_tile, 0)

    blocks = masks + [0]
    for turn in range(rounds):
        final = turn == rounds - 1
        for mask in blocks:
            arrived(turn, mask, range(4))
        lag = 2
        for step in range(len(blocks) + lag):
            if step < len(blocks):
                arrived(turn, blocks[step], [4])
                attend(turn, blocks[step])
                strip_copy(turn, blocks[step]).start()
            if step >= lag:
                mix(turn, blocks[step - lag])
        if turn + 2 < rounds:
            send_keys(turn + 2)
            send_queries(turn + 2)
        if turn >= 1 and not final:
            pass_on(turn - 1, blocks)
            if turn == 1:
                for other in range(rounds):
                    weight_copy(other).wait()
            for mask in blocks:
                pass_copy(turn - 1, mask).wait_recv()
            project(turn - 1, (0, 1))

    final = rounds - 1
    pass_on(final - 1, blocks)
    pass_on(final, [0])
    for mask in blocks:
        pass_copy(final - 1, mask).wait_recv()
    project(final - 1, (0, 1))
    pass_on(final, masks[::-1])
    project(final, (0,))
    for mask in blocks:
        pass_copy(final, mask).wait_recv()
    project(final, (1,))

    for turn in range(rounds):
        for mask in blocks:
            strip_copy(turn, mask).wait_send()
            pass_copy(turn, mask).wait_send()
            if mask != 0:
                back_copy(turn, mask).wait_send()
                for copy in moves(turn, mask):
                    copy.wait_send()
    for mask in masks:
        blend_copy(mask).wait_send()


def on_device_by_heads(query, key_image, value_image, key_text, value_text, prompt_ids, blend, w_out):
    count = lax.axis_size("seq")
    image_rows, text_rows = query.shape[1], key_text.shape[1]
    rounds = query.shape[2] // HEAD_DIM // count
    all_image = count * image_rows
    key_rows = all_image + -(-count * text_rows // 128) * 128
    strip_rows = image_rows // WCOLS
    window_strip = (rounds, count * strip_rows * STRIDE, HEAD_DIM)
    anywhere = pl.BlockSpec(memory_space=pltpu.HBM)
    vmem = pl.BlockSpec(memory_space=pltpu.VMEM)
    dma = pltpu.SemaphoreType.DMA
    operands = [
        pltpu.with_memory_space_constraint(operand, pltpu.HBM)
        for operand in (query, key_image, key_text, value_image, value_text, prompt_ids, blend, w_out)
    ]
    out = pl.pallas_call(
        functools.partial(window_kernel, count, rounds),
        out_shape=jax.ShapeDtypeStruct((strip_rows, 2, STRIDE, w_out.shape[1]), jnp.bfloat16),
        in_specs=[anywhere] * 8,
        out_specs=vmem,
        scratch_shapes=[
            pltpu.VMEM((rounds, all_image, HEAD_DIM), jnp.bfloat16),
            pltpu.VMEM((rounds, key_rows, HEAD_DIM), jnp.bfloat16),
            pltpu.VMEM((rounds, key_rows, HEAD_DIM), jnp.bfloat16),
            pltpu.VMEM(window_strip, jnp.bfloat16),
            pltpu.VMEM(window_strip, jnp.bfloat16),
            pltpu.VMEM(window_strip, jnp.bfloat16),
            pltpu.VMEM(window_strip, jnp.bfloat16),
            pltpu.VMEM((count, 8, image_rows), jnp.float32),
            pltpu.VMEM((2, strip_rows * STRIDE, query.shape[2]), jnp.bfloat16),
            pltpu.VMEM(w_out.shape, jnp.bfloat16),
            pltpu.VMEM((image_rows, w_out.shape[1]), jnp.float32),
            dma((rounds, count - 1, 5)),
            dma((rounds, count - 1, 5)),
            dma((rounds, 5)),
            dma((count - 1,)),
            dma((count - 1,)),
            dma((rounds, count)),
            dma((rounds, count)),
            dma((rounds, count - 1)),
            dma((rounds, count - 1)),
            dma((rounds,)),
            dma((rounds, count)),
            dma((rounds, count)),
            dma((rounds,)),
            pltpu.VMEM(prompt_ids.shape, prompt_ids.dtype),
            pltpu.VMEM(blend.shape, blend.dtype),
            dma((2,)),
        ],
        compiler_params=pltpu.CompilerParams(
            collective_id=0, has_side_effects=True, vmem_limit_bytes=VMEM_GRANT
        ),
    )(*operands)
    return out.reshape(1, image_rows, w_out.shape[1])


def solution(mesh):
    seq_count = mesh.shape["seq"]
    by_heads = seq_count > 1 and seq_count & (seq_count - 1) == 0 and HEADS % seq_count == 0
    placed = (
        P(("pano", "win"), "seq", None),
        P(("pano", "win"), "seq", None),
        P(("pano", "win"), "seq", None),
        P(("pano", "win"), "seq", None),
        P(("pano", "win"), "seq", None),
        P(("pano", "win"), None),
        P(("pano", "win"), "seq"),
        P(),
    )
    return jax.shard_map(
        on_device_by_heads if by_heads else on_device,
        mesh=mesh,
        in_specs=placed,
        out_specs=P(("pano", "win"), "seq", None),
        check_vma=False,
    )
```

```python
import functools

import jax
import jax.numpy as jnp
from jax import lax
from jax.experimental import pallas as pl
from jax.experimental.pallas import tpu as pltpu
from jax.sharding import PartitionSpec as P

HEADS = 12
HEAD_DIM = 128
WCOLS = 64
ROWS_DEV = 3
STRIDE = 32


blend_total = 16.0


def swapped(block, axis, stride):
    count = lax.axis_size(axis)
    route = []
    for low in range(count):
        high = low | 1 << stride
        if high != low and high < count:
            route += [(low, high), (high, low)]
    return lax.ppermute(block, axis, route)


def shifted(block, axis, distance):
    devices = range(lax.axis_size(axis))
    route = [((i - distance) % len(devices), i) for i in devices]
    return lax.ppermute(block, axis, route)


def regroup(stacked, bit_count):
    row_count = stacked.shape[0]
    carried = stacked.reshape(row_count, 1 << bit_count, -1)
    position = lax.axis_index("seq")
    for bit_index in range(bit_count):
        own_bit = position >> bit_index & 1
        paired = carried.reshape(carried.shape[0], carried.shape[1] // 2, 2, carried.shape[2])
        kept_half = lax.dynamic_index_in_dim(paired, own_bit, 2, keepdims=False)
        sent_half = lax.dynamic_index_in_dim(paired, 1 - own_bit, 2, keepdims=False)
        received = swapped(sent_half, "seq", bit_index)
        lower_half = jnp.where(own_bit == 0, kept_half, received)
        upper_half = jnp.where(own_bit == 0, received, kept_half)
        carried = jnp.concatenate([lower_half, upper_half], axis=0)
    return carried.reshape(carried.shape[0], -1)


def ungroup(attended, bit_count):
    carried = attended.reshape(attended.shape[0], 1, attended.shape[1])
    position = lax.axis_index("seq")
    for bit_index in reversed(range(bit_count)):
        own_bit = position >> bit_index & 1
        halves = carried.reshape(2, carried.shape[0] // 2, carried.shape[1], carried.shape[2])
        kept_half = lax.dynamic_index_in_dim(halves, own_bit, 0, keepdims=False)
        sent_half = lax.dynamic_index_in_dim(halves, 1 - own_bit, 0, keepdims=False)
        received = swapped(sent_half, "seq", bit_index)
        lower_half = jnp.where(own_bit == 0, kept_half, received)
        upper_half = jnp.where(own_bit == 0, received, kept_half)
        stacked = jnp.stack([lower_half, upper_half], axis=2)
        carried = stacked.reshape(kept_half.shape[0], -1, kept_half.shape[2])
    return carried.reshape(carried.shape[0], -1)


def absorb(carried, key_value, valid_keys, queries, head_count):
    running, denominator, numerator = carried
    keys_block = key_value[0].reshape(key_value.shape[1], head_count, HEAD_DIM)
    values_block = key_value[1].reshape(key_value.shape[1], head_count, HEAD_DIM)
    scores = jnp.einsum(
        "qhd,khd->qhk", queries, keys_block, preferred_element_type=jnp.float32
    ) * HEAD_DIM ** (-0.5)
    scores = jnp.where(valid_keys[None, None, :], scores, -jnp.inf)
    updated = jnp.maximum(running, jnp.max(scores, axis=2))
    rescale = jnp.exp(running - updated)
    weights = jnp.exp(scores - updated[:, :, None])
    denominator = denominator * rescale + jnp.sum(weights, axis=2)
    product = jnp.einsum(
        "qhk,khd->qhd",
        weights.astype(jnp.bfloat16),
        values_block,
        preferred_element_type=jnp.float32,
    )
    numerator = numerator * rescale[:, :, None] + product
    return (updated, denominator, numerator)


def pass_strips(window_rows):
    from_prev = shifted(window_rows[:, STRIDE:], "win", 1)
    from_next = shifted(window_rows[:, :STRIDE], "win", -1)
    return (from_prev, from_next)


def project_rows(features, w_out):
    flat_rows = features.reshape(-1, features.shape[-1])
    result = jnp.dot(flat_rows, w_out, preferred_element_type=jnp.float32).astype(jnp.bfloat16)
    return result.reshape(ROWS_DEV, -1, w_out.shape[1])


def on_device(query, key_image, value_image, key_text, value_text, prompt_ids, blend, w_out):
    bit_count = 2
    group_size = 1 << bit_count
    image_rows = query.shape[1]
    text_rows = key_text.shape[1]
    key_rows = image_rows + text_rows
    head_count = HEADS // group_size
    stacked = jnp.concatenate(
        [query[0], key_image[0], key_text[0], value_image[0], value_text[0]], axis=0
    )
    grouped = regroup(stacked, bit_count).reshape(group_size, image_rows + 2 * key_rows, -1)
    queries = grouped[:, :image_rows].reshape(group_size * image_rows, head_count, HEAD_DIM)
    keys_grouped = grouped[:, image_rows : image_rows + key_rows].reshape(group_size * key_rows, -1)
    values_grouped = grouped[:, image_rows + key_rows :].reshape(group_size * key_rows, -1)
    key_value = jnp.stack([keys_grouped, values_grouped])
    seq_count = lax.axis_size("seq")
    text_valid = prompt_ids[0].reshape(seq_count, text_rows) != 0
    key_valid = jnp.concatenate([jnp.ones((seq_count, image_rows), jnp.bool_), text_valid], axis=1)
    group_count = seq_count // group_size
    own_group = lax.axis_index("seq") // group_size

    def valid_for(source):
        return lax.dynamic_slice_in_dim(key_valid, source * group_size, group_size, 0).reshape(-1)

    query_count = group_size * image_rows
    initial = (
        jnp.full((query_count, head_count), -jnp.inf, jnp.float32),
        jnp.zeros((query_count, head_count), jnp.float32),
        jnp.zeros((query_count, head_count, HEAD_DIM), jnp.float32),
    )
    carried = absorb(initial, key_value, valid_for(own_group), queries, head_count)

    def one_turn(turn_index, loop_state):
        current, moving = loop_state
        moving = shifted(moving, "seq", group_size)
        source = (own_group - turn_index) % group_count
        return (absorb(current, moving, valid_for(source), queries, head_count), moving)

    carried, key_value = lax.fori_loop(1, group_count, one_turn, (carried, key_value))
    running, denominator, numerator = carried
    attended = (numerator / denominator[:, :, None]).astype(jnp.bfloat16).reshape(query_count, -1)
    attended = ungroup(attended, bit_count)
    got_prev, got_next = pass_strips(attended.reshape(ROWS_DEV, WCOLS, -1))
    projected = project_rows(attended, w_out)
    from_prev = project_rows(got_prev, w_out)
    from_next = project_rows(got_next, w_out)
    weight_own = blend[0].reshape(ROWS_DEV, WCOLS, 1).astype(jnp.float32)
    partner = jnp.concatenate([from_prev, from_next], axis=1).astype(jnp.float32)
    joined = (
        weight_own * projected.astype(jnp.float32) + (blend_total - weight_own) * partner
    ) / blend_total
    return joined.astype(jnp.bfloat16).reshape(1, -1, joined.shape[-1])


MESH = pl.DeviceIdType.MESH
LOG2E = 1.4426950408889634


VMEM_GRANT = 28 * 1024 * 1024


def partner_of(position, mask):
    bit = 1
    while bit <= mask:
        if mask & bit:
            position = position + (1 - 2 * ((position // bit) % 2)) * bit
        bit *= 2
    return position


def window_kernel(
    count, rounds, query, key_image, key_text, value_image, value_text, prompt_ids, blend, w_out,
    out, queries, keys, values, left, right, prev_right, mixed, blends, features, weights, partial,
    send_sem, recv_sem, own_sem, blend_send, blend_recv, strip_send, strip_recv,
    back_send, back_recv, back_own, pass_send, pass_recv, weight_sem, ids_held, blend_held, small_sem,
):
    image_rows = query.shape[1]
    text_rows = key_text.shape[1]
    all_image = count * image_rows
    strip_rows = image_rows // WCOLS
    strip_size = strip_rows * STRIDE
    pad_rows = keys.shape[1] - all_image - count * text_rows
    width = count * HEAD_DIM
    me = lax.axis_index("seq")
    windows = lax.axis_size("win")
    window = lax.axis_index("win")
    after = lax.rem(window + 1, windows)
    before = lax.rem(window + windows - 1, windows)
    masks = list(range(count - 1, 0, -1))

    small = [
        pltpu.make_async_copy(prompt_ids, ids_held, small_sem.at[0]),
        pltpu.make_async_copy(blend, blend_held, small_sem.at[1]),
    ]
    for copy in small:
        copy.start()
    barrier = pltpu.get_barrier_semaphore()
    for mask in masks:
        pl.semaphore_signal(barrier, inc=1, device_id={"seq": partner_of(me, mask)}, device_id_type=MESH)
    for other in (after, before):
        pl.semaphore_signal(barrier, inc=1, device_id={"win": other}, device_id_type=MESH)

    def pieces(turn, head, place):
        columns = pl.ds(pl.multiple_of(head * HEAD_DIM, HEAD_DIM), HEAD_DIM)
        image = pl.ds(pl.multiple_of(place * image_rows, image_rows), image_rows)
        text = pl.ds(pl.multiple_of(all_image + place * text_rows, text_rows), text_rows)
        return (
            (key_image.at[0, :, columns], keys.at[turn, image, :]),
            (key_text.at[0, :, columns], keys.at[turn, text, :]),
            (value_image.at[0, :, columns], values.at[turn, image, :]),
            (value_text.at[0, :, columns], values.at[turn, text, :]),
            (query.at[0, :, columns], queries.at[turn, image, :]),
        )

    def moves(turn, mask, arriving=False, indices=range(5)):
        other = partner_of(me, mask)
        made = pieces(turn, turn * count + other, other if arriving else me)
        if mask == 0:
            return [pltpu.make_async_copy(s, t, own_sem.at[turn, i]) for i, (s, t) in enumerate(made) if i in indices]
        return [
            pltpu.make_async_remote_copy(
                s, t, send_sem.at[turn, mask - 1, i], recv_sem.at[turn, mask - 1, i],
                device_id={"seq": other}, device_id_type=MESH)
            for i, (s, t) in enumerate(made)
            if i in indices
        ]

    def send_keys(turn):
        for index in range(4):
            for mask in masks:
                moves(turn, mask, indices=[index])[0].start()

    def send_queries(turn):
        for mask in masks:
            moves(turn, mask, indices=[4])[0].start()

    def arrived(turn, mask, indices):
        for copy in moves(turn, mask, True, indices):
            if mask == 0:
                copy.wait()
            else:
                copy.wait_recv()

    def blend_copy(mask, arriving=False):
        other = partner_of(me, mask)
        place = other if arriving else me
        return pltpu.make_async_remote_copy(
            blends.at[place], blends.at[place], blend_send.at[mask - 1], blend_recv.at[mask - 1],
            device_id={"seq": other}, device_id_type=MESH)

    def strip_place(mask):
        place = partner_of(me, mask)
        return pl.ds(pl.multiple_of(place * strip_size, strip_size), strip_size)

    def strip_copy(turn, mask):
        rows = strip_place(mask)
        return pltpu.make_async_remote_copy(
            right.at[turn, rows], prev_right.at[turn, rows], strip_send.at[turn, mask], strip_recv.at[turn, mask],
            device_id={"win": after}, device_id_type=MESH)

    def head_columns(turn, place):
        return pl.ds(pl.multiple_of((turn * count + place) * HEAD_DIM, HEAD_DIM), HEAD_DIM)

    def back_copy(turn, mask, arriving=False):
        other = partner_of(me, mask)
        source = mixed.at[turn, strip_place(mask)]
        target = features.at[0, :, head_columns(turn, other if arriving else me)]
        if mask == 0:
            return pltpu.make_async_copy(source, target, back_own.at[turn])
        return pltpu.make_async_remote_copy(
            source, target, back_send.at[turn, mask - 1], back_recv.at[turn, mask - 1],
            device_id={"seq": other}, device_id_type=MESH)

    def pass_copy(turn, mask):
        columns = head_columns(turn, partner_of(me, mask))
        return pltpu.make_async_remote_copy(
            features.at[0, :, columns], features.at[1, :, columns], pass_send.at[turn, mask], pass_recv.at[turn, mask],
            device_id={"win": before}, device_id_type=MESH)

    def weight_copy(turn):
        rows = pl.ds(turn * width, width)
        return pltpu.make_async_copy(w_out.at[rows, :], weights.at[rows, :], weight_sem.at[turn])

    for copy in small:
        copy.wait()
    blends[me] = jnp.broadcast_to(blend_held[...].astype(jnp.float32), (8, image_rows))
    pl.semaphore_wait(barrier, len(masks) + 2)
    for turn in range(min(2, rounds)):
        send_keys(turn)
        send_queries(turn)
        if turn == 0:
            for mask in masks:
                blend_copy(mask).start()
    for turn in range(rounds):
        for copy in moves(turn, 0):
            copy.start()
    for turn in range(rounds):
        weight_copy(turn).start()

    if pad_rows:
        zeros = jnp.zeros((rounds, pad_rows, HEAD_DIM), keys.dtype)
        keys[:, all_image + count * text_rows :, :] = zeros
        values[:, all_image + count * text_rows :, :] = zeros
    given = jnp.where(ids_held[...] != 0, 0.0, -jnp.inf).astype(jnp.float32)
    if pad_rows:
        given = jnp.concatenate([given, jnp.full((1, pad_rows), -jnp.inf, jnp.float32)], axis=1)
    scale = HEAD_DIM ** -0.5 * LOG2E
    contract = (((1,), (1,)), ((), ()))

    def attend(turn, mask):
        place = partner_of(me, mask)
        held = queries[turn, pl.ds(pl.multiple_of(place * image_rows, image_rows), image_rows), :]
        image_scores = lax.dot_general(held, keys[turn, :all_image, :], contract, preferred_element_type=jnp.float32)
        text_scores = lax.dot_general(held, keys[turn, all_image:, :], contract, preferred_element_type=jnp.float32) + given
        peak = jnp.maximum(jnp.max(image_scores, axis=1, keepdims=True), jnp.max(text_scores, axis=1, keepdims=True))
        image_weights = jnp.exp2((image_scores - peak) * scale)
        text_weights = jnp.exp2((text_scores - peak) * scale)
        total = jnp.sum(image_weights, axis=1, keepdims=True) + jnp.sum(text_weights, axis=1, keepdims=True)
        product = jnp.dot(image_weights.astype(jnp.bfloat16), values[turn, :all_image, :], preferred_element_type=jnp.float32)
        product += jnp.dot(text_weights.astype(jnp.bfloat16), values[turn, all_image:, :], preferred_element_type=jnp.float32)
        attended = (product * (1.0 / total)).astype(jnp.bfloat16).reshape(strip_rows, WCOLS, HEAD_DIM)
        left[turn, strip_place(mask), :] = attended[:, :STRIDE].reshape(strip_size, HEAD_DIM)
        right[turn, strip_place(mask), :] = attended[:, STRIDE:].reshape(strip_size, HEAD_DIM)

    def own_weight(mask):
        token = lax.broadcasted_iota(jnp.int32, (strip_size, image_rows), 1)
        spot = lax.broadcasted_iota(jnp.int32, (strip_size, image_rows), 0)
        chosen = token == (spot // STRIDE) * WCOLS + spot % STRIDE
        spread = jnp.where(chosen, blends[partner_of(me, mask)][:1, :], 0.0).astype(jnp.bfloat16)
        return jnp.dot(spread, jnp.ones((image_rows, HEAD_DIM), jnp.bfloat16), preferred_element_type=jnp.float32)

    def mix(turn, mask):
        if turn == 0 and mask != 0:
            blend_copy(mask, True).wait_recv()
        strip_copy(turn, mask).wait_recv()
        own = own_weight(mask)
        mine = left[turn, strip_place(mask), :].astype(jnp.float32)
        theirs = prev_right[turn, strip_place(mask), :].astype(jnp.float32)
        mixed[turn, strip_place(mask), :] = ((own * mine + (blend_total - own) * theirs) * (1.0 / blend_total)).astype(jnp.bfloat16)
        back_copy(turn, mask).start()

    def pass_on(turn, order):
        for mask in order:
            copy = back_copy(turn, mask, True)
            if mask == 0:
                copy.wait()
            else:
                copy.wait_recv()
            pass_copy(turn, mask).start()

    tile = 512

    def project(turn, halves):
        first, final = turn == 0, turn == rounds - 1
        low, high = halves[0] * strip_size, (halves[-1] + 1) * strip_size
        rows = features[halves[0] : halves[-1] + 1, :, turn * width : (turn + 1) * width].reshape(high - low, width)

        def one_tile(index, carry):
            columns = pl.ds(pl.multiple_of(index * tile, tile), tile)
            result = jnp.dot(rows, weights[turn * width : (turn + 1) * width, columns], preferred_element_type=jnp.float32)
            if not first:
                result = result + partial[low:high, columns]
            if not final:
                partial[low:high, columns] = result
            else:
                result = result.astype(jnp.bfloat16).reshape(len(halves), strip_rows, STRIDE, tile)
                for place, half in enumerate(halves):
                    out[:, half, :, columns] = result[place]
            return carry

        lax.fori_loop(0, weights.shape[1] // tile, one_tile, 0)

    blocks = masks + [0]
    for turn in range(rounds):
        final = turn == rounds - 1
        for mask in blocks:
            arrived(turn, mask, range(4))
        lag = min(3, count)
        for step in range(len(blocks) + lag):
            if step < len(blocks):
                arrived(turn, blocks[step], [4])
                attend(turn, blocks[step])
                strip_copy(turn, blocks[step]).start()
            if step == len(blocks) and final:
                pass_on(turn - 1, blocks)
            if step >= lag:
                mix(turn, blocks[step - lag])
        if turn + 2 < rounds:
            send_keys(turn + 2)
            send_queries(turn + 2)
        if turn >= 1 and not final:
            pass_on(turn - 1, blocks)
            if turn == 1:
                for other in range(rounds):
                    weight_copy(other).wait()
            for mask in blocks:
                pass_copy(turn - 1, mask).wait_recv()
            project(turn - 1, (0, 1))

    final = rounds - 1
    pass_on(final, [0])
    for mask in blocks:
        pass_copy(final - 1, mask).wait_recv()
    project(final - 1, (0, 1))
    pass_on(final, masks[::-1])
    project(final, (0,))
    for mask in blocks:
        pass_copy(final, mask).wait_recv()
    project(final, (1,))

    for turn in range(rounds):
        for mask in blocks:
            strip_copy(turn, mask).wait_send()
            pass_copy(turn, mask).wait_send()
            if mask != 0:
                back_copy(turn, mask).wait_send()
                for copy in moves(turn, mask):
                    copy.wait_send()
    for mask in masks:
        blend_copy(mask).wait_send()


def on_device_by_heads(query, key_image, value_image, key_text, value_text, prompt_ids, blend, w_out):
    count = lax.axis_size("seq")
    image_rows, text_rows = query.shape[1], key_text.shape[1]
    rounds = query.shape[2] // HEAD_DIM // count
    all_image = count * image_rows
    key_rows = all_image + -(-count * text_rows // 128) * 128
    strip_rows = image_rows // WCOLS
    window_strip = (rounds, count * strip_rows * STRIDE, HEAD_DIM)
    anywhere = pl.BlockSpec(memory_space=pltpu.HBM)
    vmem = pl.BlockSpec(memory_space=pltpu.VMEM)
    dma = pltpu.SemaphoreType.DMA
    operands = [
        pltpu.with_memory_space_constraint(operand, pltpu.HBM)
        for operand in (query, key_image, key_text, value_image, value_text, prompt_ids, blend, w_out)
    ]
    out = pl.pallas_call(
        functools.partial(window_kernel, count, rounds),
        out_shape=jax.ShapeDtypeStruct((strip_rows, 2, STRIDE, w_out.shape[1]), jnp.bfloat16),
        in_specs=[anywhere] * 8,
        out_specs=vmem,
        scratch_shapes=[
            pltpu.VMEM((rounds, all_image, HEAD_DIM), jnp.bfloat16),
            pltpu.VMEM((rounds, key_rows, HEAD_DIM), jnp.bfloat16),
            pltpu.VMEM((rounds, key_rows, HEAD_DIM), jnp.bfloat16),
            pltpu.VMEM(window_strip, jnp.bfloat16),
            pltpu.VMEM(window_strip, jnp.bfloat16),
            pltpu.VMEM(window_strip, jnp.bfloat16),
            pltpu.VMEM(window_strip, jnp.bfloat16),
            pltpu.VMEM((count, 8, image_rows), jnp.float32),
            pltpu.VMEM((2, strip_rows * STRIDE, query.shape[2]), jnp.bfloat16),
            pltpu.VMEM(w_out.shape, jnp.bfloat16),
            pltpu.VMEM((image_rows, w_out.shape[1]), jnp.float32),
            dma((rounds, count - 1, 5)),
            dma((rounds, count - 1, 5)),
            dma((rounds, 5)),
            dma((count - 1,)),
            dma((count - 1,)),
            dma((rounds, count)),
            dma((rounds, count)),
            dma((rounds, count - 1)),
            dma((rounds, count - 1)),
            dma((rounds,)),
            dma((rounds, count)),
            dma((rounds, count)),
            dma((rounds,)),
            pltpu.VMEM(prompt_ids.shape, prompt_ids.dtype),
            pltpu.VMEM(blend.shape, blend.dtype),
            dma((2,)),
        ],
        compiler_params=pltpu.CompilerParams(
            collective_id=0, has_side_effects=True, vmem_limit_bytes=VMEM_GRANT
        ),
    )(*operands)
    return out.reshape(1, image_rows, w_out.shape[1])


def solution(mesh):
    seq_count = mesh.shape["seq"]
    by_heads = seq_count > 1 and seq_count & (seq_count - 1) == 0 and HEADS % seq_count == 0
    placed = (
        P(("pano", "win"), "seq", None),
        P(("pano", "win"), "seq", None),
        P(("pano", "win"), "seq", None),
        P(("pano", "win"), "seq", None),
        P(("pano", "win"), "seq", None),
        P(("pano", "win"), None),
        P(("pano", "win"), "seq"),
        P(),
    )
    return jax.shard_map(
        on_device_by_heads if by_heads else on_device,
        mesh=mesh,
        in_specs=placed,
        out_specs=P(("pano", "win"), "seq", None),
        check_vma=False,
    )
```
